128 devices in a mesh: cfg: 2 (over core), req: 4 (over y), seq: 16 (over z, x).
Axes of the slice: x: 4, y: 4, z: 4, core: 2. Of those that a mesh axis runs over, the one named last changes fastest.
Arguments:
- latent: float32 [8, 2048, 64], P('req', 'seq'), may hold values from -6 to 6
- hidden_in: bfloat16 [2, 8, 2048, 2432], P('cfg', 'req', 'seq'), may hold values from -25 to 25
- img_query: bfloat16 [2, 8, 2048, 2432], P('cfg', 'req', 'seq'), may hold values from -10 to 10
- img_key: bfloat16 [2, 8, 2048, 2432], P('cfg', 'req', 'seq'), may hold values from -10 to 10
- img_value: bfloat16 [2, 8, 2048, 2432], P('cfg', 'req', 'seq'), may hold values from -6 to 6
- txt_key: bfloat16 [2, 8, 160, 2432], P('cfg', 'req', 'seq'), may hold values from -10 to 10
- txt_value: bfloat16 [2, 8, 160, 2432], P('cfg', 'req', 'seq'), may hold values from -6 to 6
- text_len: int32 [2, 8], P('cfg', 'req'), may hold values from 38 to 154, as said below
- head_slot: int32 [38], replicated, may hold values from 0 to 47, as said below
- out_weight: bfloat16 [2432, 2432], replicated, may hold values from -0.125 to 0.125
- out_bias: float32 [2432], replicated, may hold values from -3 to 3
- attn_gate: float32 [2, 8, 2432], P('cfg', 'req'), may hold values from 0.5 to 2
- final_mod: float32 [2, 8, 2, 2432], P('cfg', 'req'), may hold values from -3 to 3
- final_weight: bfloat16 [2432, 64], replicated, may hold values from -0.125 to 0.125
- final_bias: float32 [64], replicated, may hold values from -3 to 3
- timesteps: int32 [8], P('req'), may hold values from 1 to 28
- guidance: float32 [8], P('req'), may hold values from 2.5 to 6
Outputs:
- velocity: float32 [8, 2048, 64], P('req', 'seq')
- latent_next: float32 [8, 2048, 64], P('req', 'seq')
- hidden_norms: float32 [2, 8], P('cfg', 'req')
- max_logits: float32 [48], P('seq')
The draws below stay inside these ranges and needn't reach their ends.
Inputs may be any that keep to these rules, and one draw needn't show every extreme that they name: `head_slot`: distinct heads take distinct slots; slots j * 3 to (j + 1) * 3 - 1 belong to index j of seq, and every index holds 3 heads or one fewer. Text positions below text_len are live; some half and request has exactly 154 live text tokens.
All inputs are finite; a program needn't handle non-finite values.
Results may differ from the reference program's by a relative error of at most 0.0032.
Values may be sent and summed in bfloat16 or wider, within the bound.
No kernel may reach another device: no remote copies, remote signals or barrier semaphores. Data moves between devices by JAX's collectives and lax.ppermute only.
A program may use at most 128 MiB of HBM per device.

```python
import math
import jax
import jax.numpy as jnp
from jax import lax

HEADS = 38
HD = 64
D = 2432
C_OUT = 64
IMG = 2048
TXT_LIVE = 154
TXT = 160
REQS = 8
STEPS = 28
HSLOT = 3
SLOTS = 48
N_SEQ = 16


def base_noise(noise_key, shape):
    return jnp.clip(jax.random.normal(noise_key, shape), -4.0, 4.0)


def draw_img_query(key, part):
    own_key = jax.random.fold_in(key, 31)
    noise_key, scale_key = jax.random.split(own_key)
    head_scale = jnp.exp(jax.random.uniform(scale_key, (2, REQS, 1, HEADS, 1), minval=0.0, maxval=math.log(1.8)))
    query_draw = (base_noise(noise_key, (2, REQS, IMG, HEADS, HD)) * head_scale).reshape(2, REQS, IMG, D)
    return query_draw.astype(jnp.bfloat16)


def draw_img_key(key, part):
    own_key = jax.random.fold_in(key, 37)
    key_draw = 1.2 * base_noise(own_key, (2, REQS, IMG, D))
    return key_draw.astype(jnp.bfloat16)


def draw_txt_key(key, part):
    own_key = jax.random.fold_in(key, 41)
    return (1.5 * base_noise(own_key, (2, REQS, TXT, D))).astype(jnp.bfloat16)


def draw_hidden_in(key, part):
    own_key = jax.random.fold_in(key, 43)
    noise_key, column_key = jax.random.split(own_key, 2)
    fraction = (jnp.arange(IMG, dtype=jnp.float32) / (IMG - 1))[None, None, :, None]
    column = jnp.exp(jax.random.uniform(column_key, (1, 1, 1, D), minval=0.0, maxval=math.log(10.0)))
    noise = jnp.clip(jax.random.normal(noise_key, (2, REQS, IMG, D)), -4.0, 4.0)
    result = 0.1 * noise * jnp.power(3.0, fraction) * column
    return result.astype(jnp.bfloat16)


def draw_text_len(key, part):
    own_key = jax.random.fold_in(key, 13)
    len_key, pick_key = jax.random.split(own_key)
    lengths = jax.random.randint(len_key, (2 * REQS,), TXT_LIVE // 4, TXT_LIVE + 1)
    chosen = jax.random.randint(pick_key, (), 0, 2 * REQS)
    other = (chosen + 1) % (2 * REQS)
    pair_ids = jnp.arange(2 * REQS, dtype=jnp.int32)
    lengths = jnp.where(pair_ids == chosen, TXT_LIVE, lengths)
    lengths = jnp.where(pair_ids == other, TXT_LIVE // 4, lengths)
    return lengths.reshape(2, REQS).astype(jnp.int32)


def draw_head_slot(key, part):
    own_key = jax.random.fold_in(key, 11)
    order_key, shard_key = jax.random.split(own_key)
    head_order = jax.random.permutation(order_key, HEADS)
    shard_rank = jnp.concatenate([jax.random.permutation(shard_key, N_SEQ - 1) + 1, jnp.zeros((1,), jnp.int32)])
    base_count = HEADS // N_SEQ
    extra_count = HEADS % N_SEQ
    slot_ids = jnp.arange(SLOTS, dtype=jnp.int32)
    owner = slot_ids // HSLOT
    within = slot_ids % HSLOT
    slot_used = (within < base_count) | (shard_rank[owner] < extra_count)
    used_rank = jnp.cumsum(slot_used.astype(jnp.int32)) - 1
    rank_ids = jnp.arange(HEADS, dtype=jnp.int32)
    hit_table = slot_used[None, :] & (used_rank[None, :] == rank_ids[:, None])
    slot_of_rank = jnp.sum(jnp.where(hit_table, slot_ids[None, :], 0), axis=1)
    table = jnp.zeros((HEADS,), jnp.int32).at[head_order].set(slot_of_rank)
    return table.astype(jnp.int32)


def set_ends(drawn, rng, smallest, top_value):
    shape = drawn.shape
    place = [jax.random.randint(jax.random.fold_in(rng, axis), (), 0, shape[axis]) for axis in range(len(shape))]
    drawn = drawn.at[tuple(place)].set(smallest)
    longest = shape.index(max(shape))
    place[longest] = (place[longest] + 1) % shape[longest]
    return drawn.at[tuple(place)].set(top_value)


def shard_levels(key, dims, cuts, low, largest):
    loudness, own = 1.0, jax.random.fold_in(key, 6)
    for dim, shards_of in cuts:
        steps = jnp.exp(jax.random.uniform(jax.random.fold_in(own, dim), (shards_of,), jnp.float32, low / len(cuts), largest / len(cuts)))
        loudness = loudness * jnp.repeat(steps, dims[dim] // shards_of).reshape([-1 if axis == dim else 1 for axis in range(len(dims))])
    return loudness


def normal_values(stream_key, dims, spread, limit, cuts=(), kind=jnp.bfloat16):
    values = jax.random.normal(stream_key, dims, jnp.float32) * spread
    if len(cuts) > 0:
        values = shard_levels(stream_key, dims, cuts, -0.22, 0.18) * values
    return jnp.clip(values, min=-limit, max=limit).astype(kind)


def setup_inputs(seed: int = 0) -> dict:
    streams_of = jax.random.split(jax.random.key(seed), 18)
    return {
        "latent": normal_values(streams_of[0], (REQS, IMG, C_OUT), 1.0, 6.0, ((0, 4), (1, 16)), jnp.float32),
        "hidden_in": draw_hidden_in(jax.random.fold_in(streams_of[17], 71), 0),
        "img_query": draw_img_query(jax.random.fold_in(streams_of[17], 71), 0),
        "img_key": draw_img_key(jax.random.fold_in(streams_of[17], 71), 0),
        "img_value": normal_values(streams_of[4], (2, REQS, IMG, D), 1.0, 6.0, ((0, 2), (1, 4), (2, 16))),
        "txt_key": draw_txt_key(jax.random.fold_in(streams_of[17], 71), 0),
        "txt_value": normal_values(streams_of[6], (2, REQS, TXT, D), 1.0, 6.0, ((0, 2), (1, 4), (2, 16))),
        "text_len": draw_text_len(jax.random.fold_in(streams_of[17], 71), 0),
        "head_slot": draw_head_slot(jax.random.fold_in(streams_of[17], 71), 0),
        "out_weight": normal_values(streams_of[9], (D, D), D ** -0.5, 0.125),
        "out_bias": normal_values(streams_of[10], (D,), 0.5, 3.0, (), jnp.float32),
        "attn_gate": jnp.clip(jnp.exp(math.log(2.0) - 1.3862944 * jax.random.uniform(streams_of[11], (2, REQS, D), jnp.float32) ** shard_levels(streams_of[11], (2, REQS, D), ((0, 2), (1, 4)), -0.2, 0.2)), 0.5, 2.0),
        "final_mod": normal_values(streams_of[12], (2, REQS, 2, D), 0.5, 3.0, ((0, 2), (1, 4)), jnp.float32),
        "final_weight": normal_values(streams_of[13], (D, C_OUT), D ** -0.5, 0.125),
        "final_bias": normal_values(streams_of[14], (C_OUT,), 0.5, 3.0, (), jnp.float32),
        "timesteps": set_ends(jax.random.randint(streams_of[15], (REQS,), 1, STEPS + 1), jax.random.fold_in(streams_of[15], 1), 1, STEPS).astype(jnp.int32),
        "guidance": jnp.clip(2.5 + 3.5 * jax.random.uniform(streams_of[16], (REQS,), jnp.float32) ** shard_levels(streams_of[16], (REQS,), ((0, 4),), -0.2, 0.2), 2.5, 6.0),
    }


masked_score = -1e+30

def sigma_of(step_idx):
    fraction = step_idx.astype(jnp.float32) / STEPS
    return 3.0 * fraction / (1.0 + 2.0 * fraction)

def attend_head(query_head, key_head, value_head, key_valid):
    scores = jnp.einsum('qd,kd->qk', query_head, key_head, preferred_element_type=jnp.float32) * (1.0 / math.sqrt(HD))
    scores = jnp.where(key_valid[None, :], scores, masked_score)
    row_top = lax.optimization_barrier(jnp.max(scores, axis=1, keepdims=True))
    weights = jnp.exp(scores - row_top)
    weights = (weights / lax.optimization_barrier(jnp.sum(weights, axis=1, keepdims=True))).astype(jnp.bfloat16)
    head_out = jnp.dot(weights, value_head, preferred_element_type=jnp.float32).astype(jnp.bfloat16)
    return (head_out, jnp.max(row_top))

def reference(latent, hidden_in, img_query, img_key, img_value, txt_key, txt_value, text_len, head_slot, out_weight, out_bias, attn_gate, final_mod, final_weight, final_bias, timesteps, guidance):

    def half_request(packed):
        hidden_row, query, key_img, value_img, key_txt, value_txt, length, gate, modul = packed
        query_heads = query.reshape(IMG, HEADS, HD).transpose(1, 0, 2)
        all_keys = jnp.concatenate([key_img, key_txt], axis=0).reshape(IMG + TXT, HEADS, HD).transpose(1, 0, 2)
        all_values = jnp.concatenate([value_img, value_txt], axis=0).reshape(IMG + TXT, HEADS, HD).transpose(1, 0, 2)
        key_valid = jnp.arange(IMG + TXT, dtype=jnp.int32) < IMG + length

        def one_head(parts):
            return attend_head(parts[0], parts[1], parts[2], key_valid)
        head_out, top_scores = lax.map(one_head, (query_heads, all_keys, all_values))
        attended = head_out.transpose(1, 0, 2).reshape(IMG, D)
        projected = jnp.dot(attended, out_weight, preferred_element_type=jnp.float32) + out_bias
        hidden = hidden_row.astype(jnp.float32) + gate[None, :] * projected
        norm_value = jnp.sqrt(jnp.mean(hidden * hidden))
        row_mean = lax.optimization_barrier(jnp.mean(hidden, axis=1, keepdims=True))
        centered = hidden - row_mean
        row_var = lax.optimization_barrier(jnp.mean(centered * centered, axis=1, keepdims=True))
        normed = (centered / jnp.sqrt(row_var + 1e-06) * (1.0 + modul[1][None, :]) + modul[0][None, :]).astype(jnp.bfloat16)
        prediction = jnp.dot(normed, final_weight, preferred_element_type=jnp.float32) + final_bias
        return (prediction, norm_value, top_scores)

    def flatten_pair(tensor):
        return tensor.reshape((2 * REQS,) + tensor.shape[2:])
    prediction, norm_values, top_scores = lax.map(half_request, (flatten_pair(hidden_in), flatten_pair(img_query), flatten_pair(img_key), flatten_pair(img_value), flatten_pair(txt_key), flatten_pair(txt_value), text_len.reshape(2 * REQS), flatten_pair(attn_gate), flatten_pair(final_mod)))
    prediction = prediction.reshape(2, REQS, IMG, C_OUT)
    scale_g = guidance[:, None, None]
    velocity = scale_g * prediction[0] + (1.0 - scale_g) * prediction[1]
    step_size = (sigma_of(timesteps - 1) - sigma_of(timesteps))[:, None, None]
    latent_next = latent + step_size * velocity
    head_peak = lax.optimization_barrier(jnp.max(top_scores, axis=0))
    max_logits = jnp.zeros((SLOTS,), jnp.float32).at[head_slot].set(head_peak)
    return (velocity, latent_next, norm_values.reshape(2, REQS), max_logits)
```

```python
import functools
import math

import jax
import jax.numpy as jnp
from jax import lax
from jax.experimental import pallas as pl
from jax.experimental.pallas import tpu as pltpu
from jax.sharding import PartitionSpec as P

STEPS = 28
LANES = 128
QT = 256
bf16 = jnp.bfloat16
f32 = jnp.float32


def sigma_of(step_idx):
    fraction = step_idx.astype(f32) / STEPS
    return 3.0 * fraction / (1.0 + 2.0 * fraction)


def pack_pairs_kernel(q_ref, k_ref, v_ref, tk_ref, tv_ref, out_ref):
    tok = q_ref.shape[2]
    txt = tk_ref.shape[2]
    for i in range(out_ref.shape[0]):
        cols = slice(i * LANES, (i + 1) * LANES)
        out_ref[i, 0:tok, :] = q_ref[0, 0, :, cols]
        out_ref[i, tok : 2 * tok, :] = k_ref[0, 0, :, cols]
        out_ref[i, 2 * tok : 3 * tok, :] = v_ref[0, 0, :, cols]
        out_ref[i, 3 * tok : 3 * tok + txt, :] = tk_ref[0, 0, :, cols]
        out_ref[i, 3 * tok + txt : 3 * tok + 2 * txt, :] = tv_ref[0, 0, :, cols]


def pack_pairs(r, q, k, v, tk, tv, shards):
    tok, txt = q.shape[2], tk.shape[2]
    rows = 3 * tok + 2 * txt
    per = 4
    img = pl.BlockSpec((1, 1, tok, per * LANES), lambda j: (0, r, 0, j))
    text = pl.BlockSpec((1, 1, txt, per * LANES), lambda j: (0, r, 0, j))
    return pl.pallas_call(
        pack_pairs_kernel,
        grid=(shards // per,),
        in_specs=[img, img, img, text, text],
        out_specs=pl.BlockSpec((per, rows, LANES), lambda j: (j, 0, 0)),
        out_shape=jax.ShapeDtypeStruct((shards, rows, LANES), bf16),
        cost_estimate=pl.CostEstimate(flops=0, bytes_accessed=4 * shards * rows * LANES, transcendentals=0),
        name="pack_pairs",
    )(q, k, v, tk, tv)


def pack_single_kernel(n_pairs, q_ref, k_ref, v_ref, tk_ref, tv_ref, out_ref):
    j = pl.program_id(0)
    tok = q_ref.shape[2]
    txt = tk_ref.shape[2]
    half = tok // 2
    hd = LANES // 2

    @pl.when(j < n_pairs)
    def _():
        for r in range(2):
            for h in range(2):
                d = 2 * r + h
                for n, ref in enumerate((q_ref, k_ref, v_ref)):
                    x = ref[0, r]
                    top, low = x[:half], x[half:]
                    if h == 0:
                        folded = jnp.concatenate([top[:, :hd], low[:, :hd]], axis=1)
                    else:
                        folded = jnp.concatenate([top[:, hd:], low[:, hd:]], axis=1)
                    out_ref[d, n * half : (n + 1) * half, :] = folded
                for n, ref in enumerate((tk_ref, tv_ref)):
                    x = ref[0, r][:, h * hd : (h + 1) * hd]
                    base = 3 * half + n * txt
                    out_ref[d, base : base + txt, :] = jnp.concatenate([x, x], axis=1)

    @pl.when(j >= n_pairs)
    def _():
        out_ref[...] = jnp.zeros_like(out_ref)


def pack_single(q, k, v, tk, tv, shards):
    tok, txt = q.shape[2], tk.shape[2]
    n_pairs = q.shape[3] // LANES - shards
    rows = 3 * (tok // 2) + 2 * txt
    last = n_pairs - 1
    img = pl.BlockSpec((1, 2, tok, LANES), lambda j: (0, 0, 0, shards + jnp.minimum(j, last)))
    text = pl.BlockSpec((1, 2, txt, LANES), lambda j: (0, 0, 0, shards + jnp.minimum(j, last)))
    return pl.pallas_call(
        functools.partial(pack_single_kernel, n_pairs),
        grid=(shards // 4,),
        in_specs=[img, img, img, text, text],
        out_specs=pl.BlockSpec((4, rows, LANES), lambda j: (j, 0, 0)),
        out_shape=jax.ShapeDtypeStruct((shards, rows, LANES), bf16),
        cost_estimate=pl.CostEstimate(flops=0, bytes_accessed=4 * shards * rows * LANES, transcendentals=0),
        name="pack_single",
    )(q, k, v, tk, tv)


def attend_kernel(folded, tok, txt, len_ref, r_ref, o_ref, top_ref, k2, vt, top):
    shards = r_ref.shape[0]
    hd = LANES // 2
    rows = tok // 2 if folded else tok
    n_img = shards * tok
    slot = 16
    n_txt = shards * slot
    t = pl.program_id(0)
    length = len_ref[0]

    @pl.when(t == 0)
    def _prep():
        for s in range(shards):
            kb = r_ref[s, rows : 2 * rows, :]
            at = slice(s * rows, (s + 1) * rows)
            k2[at, 0:LANES] = kb
            k2[at, LANES:] = kb
            if folded:
                other = jnp.concatenate([kb[:, hd:], kb[:, :hd]], axis=1)
                at2 = slice(n_img // 2 + s * rows, n_img // 2 + (s + 1) * rows)
                k2[at2, 0:LANES] = other
                k2[at2, LANES:] = other
        step = LANES // rows
        for u in range(shards // step):
            vb = r_ref[u * step : (u + 1) * step, 2 * rows : 3 * rows, :].reshape(LANES, LANES)
            vb = vb.astype(f32).T.astype(bf16)
            at = slice(u * LANES, (u + 1) * LANES)
            vt[0, 0:hd, at] = vb[:hd]
            vt[1, 0:hd, at] = vb[hd:]
            if folded:
                at2 = slice(n_img // 2 + u * LANES, n_img // 2 + (u + 1) * LANES)
                vt[0, 0:hd, at2] = vb[hd:]
                vt[1, 0:hd, at2] = vb[:hd]
        tks, tvs = [], []
        pad = jnp.zeros((slot - txt, LANES), f32)
        for s in range(shards):
            tks += [r_ref[s, 3 * rows : 3 * rows + txt, :].astype(f32), pad]
            tvs += [r_ref[s, 3 * rows + txt : 3 * rows + 2 * txt, :].astype(f32), pad]
        tkx = jnp.concatenate(tks, axis=0)
        tvx = jnp.concatenate(tvs, axis=0)
        i = lax.broadcasted_iota(jnp.int32, (n_txt, LANES), 0)
        live = ((i % slot) < txt) & ((i // slot) * txt + (i % slot) < length)
        key0 = k2[0:16, 0:LANES].astype(f32)[0:1]
        tkx = jnp.where(live, tkx, jnp.broadcast_to(key0, (n_txt, LANES))).astype(bf16)
        k2[n_img:, 0:LANES] = tkx
        k2[n_img:, LANES:] = tkx
        tvx = jnp.where(live, tvx, 0.0)
        for u in range(n_txt // LANES):
            vb = tvx[u * LANES : (u + 1) * LANES].T.astype(bf16)
            at = slice(n_img + u * LANES, n_img + (u + 1) * LANES)
            vt[0, 0:hd, at] = vb[:hd]
            vt[1, 0:hd, at] = vb[hd:]
        c = lax.broadcasted_iota(jnp.int32, (slot, n_txt), 1)
        live_t = ((c % slot) < txt) & ((c // slot) * txt + (c % slot) < length)
        ones_t = jnp.where(live_t, 1.0, 0.0).astype(bf16)
        for h in range(2):
            vt[h, hd:, 0:n_img] = jnp.ones((slot, n_img), bf16)
            vt[h, hd:, n_img:] = ones_t
        top[...] = jnp.full(top.shape, -jnp.inf, f32)

    per = QT // rows
    q = r_ref[pl.ds(t * per, per), 0:rows, :].reshape(QT, LANES).astype(f32)
    q = q * (math.log2(math.e) / math.sqrt(hd))
    lane = lax.broadcasted_iota(jnp.int32, (QT, LANES), 1)
    outs = []
    for h in range(2):
        qh = jnp.where((lane >= hd) == (h == 1), q, 0.0)
        hi = qh.astype(bf16)
        lo = (qh - hi.astype(f32)).astype(bf16)
        q2 = jnp.concatenate([hi, lo], axis=1)
        s = lax.dot_general(k2[...], q2, (((1,), (1,)), ((), ())), preferred_element_type=f32)
        m = jnp.max(s, axis=0, keepdims=True)
        p = jnp.exp2(s - m).astype(bf16)
        o = jnp.dot(vt[h], p, preferred_element_type=f32)
        outs.append(o[:hd] / o[hd : hd + 1])
        top[h : h + 1, :] = jnp.maximum(top[h : h + 1, :], m)
    out = jnp.concatenate(outs, axis=0).T.astype(bf16)
    o_ref[...] = out.reshape(per, rows, LANES)

    @pl.when(t == pl.num_programs(0) - 1)
    def _fin():
        best = jnp.max(top[...], axis=1, keepdims=True) * math.log(2.0)
        top_ref[...] = jnp.broadcast_to(best, top_ref.shape)


def attend(received, length, tok, txt, folded):
    shards, total, _ = received.shape
    rows = tok // 2 if folded else tok
    n_keys = shards * (tok + 16)
    per = QT // rows
    heads = 1 if folded else 2
    return pl.pallas_call(
        functools.partial(attend_kernel, folded, tok, txt),
        grid=(shards // per,),
        in_specs=[
            pl.BlockSpec(memory_space=pltpu.SMEM),
            pl.BlockSpec((shards, total, LANES), lambda t: (0, 0, 0)),
        ],
        out_specs=[
            pl.BlockSpec((per, rows, LANES), lambda t: (t, 0, 0)),
            pl.BlockSpec((8, LANES), lambda t: (0, 0)),
        ],
        out_shape=[
            jax.ShapeDtypeStruct((shards, rows, LANES), bf16),
            jax.ShapeDtypeStruct((8, LANES), f32),
        ],
        scratch_shapes=[
            pltpu.VMEM((n_keys, 2 * LANES), bf16),
            pltpu.VMEM((2, LANES // 2 + 16, n_keys), bf16),
            pltpu.VMEM((8, QT), f32),
        ],
        compiler_params=pltpu.CompilerParams(vmem_limit_bytes=40 * 1024 * 1024),
        cost_estimate=pl.CostEstimate(
            flops=heads * 4 * shards * tok * n_keys * LANES,
            bytes_accessed=4 * shards * total * LANES,
            transcendentals=heads * shards * tok * n_keys,
        ),
        name="attend_single" if folded else "attend_pair",
    )(length, received)


def finish_kernel(
    n_pairs, half_ref, a_ref, b_ref, c_ref, hid_ref, gate_ref, mod_ref, ob_ref, fw_ref, fb_ref, w_hbm,
    pred_ref, sq_ref, att, w, acc, sem,
):
    shards, tok, _ = a_ref.shape
    width = w.shape[0]
    hd = LANES // 2
    half = tok // 2
    edges = list(range(0, width, 4 * LANES)) + [width]
    copies = [
        pltpu.make_async_copy(w_hbm.at[lo:up, :], w.at[lo:up, :], sem.at[n])
        for n, (lo, up) in enumerate(zip(edges[:-1], edges[1:]))
    ]
    for copy in copies:
        copy.start()
    for d in range(shards):
        att[0:tok, d * LANES : (d + 1) * LANES] = a_ref[d]
        att[tok:, d * LANES : (d + 1) * LANES] = b_ref[d]
    for j in range(n_pairs):
        for r in range(2):
            x0 = c_ref[4 * j + 2 * r]
            x1 = c_ref[4 * j + 2 * r + 1]
            cols = slice((shards + j) * LANES, (shards + j + 1) * LANES)
            att[r * tok : r * tok + half, cols] = jnp.concatenate([x0[:, :hd], x1[:, :hd]], axis=1)
            att[r * tok + half : (r + 1) * tok, cols] = jnp.concatenate([x0[:, hd:], x1[:, hd:]], axis=1)
    for n, (lo, up) in enumerate(zip(edges[:-1], edges[1:])):
        copies[n].wait()
        part = jnp.dot(att[:, lo:up], w[lo:up, :], preferred_element_type=f32)
        if n == 0:
            acc[...] = part
        else:
            acc[...] += part

    step = 16
    for r in range(2):
        gate = gate_ref[0, r : r + 1, :]
        shift = mod_ref[0, r, 0:1, :]
        scale = 1.0 + mod_ref[0, r, 1:2, :]
        bias = ob_ref[...]

        def body(i, total):
            at = pl.ds(r * tok + i * step, step)
            hid = hid_ref[0, r, pl.ds(i * step, step), :].astype(f32) + gate * (acc[at, :] + bias)
            total = total + jnp.sum(hid * hid, axis=1, keepdims=True)
            mean = jnp.mean(hid, axis=1, keepdims=True)
            cen = hid - mean
            var = jnp.mean(cen * cen, axis=1, keepdims=True)
            att[at, :] = (cen / jnp.sqrt(var + 1e-6) * scale + shift).astype(bf16)
            return total

        total = lax.fori_loop(0, tok // step, body, jnp.zeros((step, 1), f32))
        sq_ref[r : r + 1, :] = jnp.broadcast_to(jnp.sum(total, axis=0, keepdims=True), (1, LANES))
        pred = jnp.dot(att[r * tok : (r + 1) * tok, :], fw_ref[...], preferred_element_type=f32)
        pred_ref[r] = half_ref[r] * (pred + fb_ref[...])


def finish(half_weight, ra, rb, rc, hidden_in, gate, mod, out_bias, final_weight, final_bias, out_weight):
    shards, tok, _ = ra.shape
    width = out_weight.shape[0]
    c_out = final_weight.shape[1]
    n_pairs = width // LANES - shards
    vmem = pl.BlockSpec(memory_space=pltpu.VMEM)
    return pl.pallas_call(
        functools.partial(finish_kernel, n_pairs),
        in_specs=[pl.BlockSpec(memory_space=pltpu.SMEM)] + [vmem] * 9 + [pl.BlockSpec(memory_space=pl.ANY)],
        out_specs=[vmem, vmem],
        out_shape=[
            jax.ShapeDtypeStruct((2, tok, c_out), f32),
            jax.ShapeDtypeStruct((8, LANES), f32),
        ],
        scratch_shapes=[
            pltpu.VMEM((2 * tok, width), bf16),
            pltpu.VMEM((width, width), bf16),
            pltpu.VMEM((2 * tok, width), f32),
            pltpu.SemaphoreType.DMA((5,)),
        ],
        compiler_params=pltpu.CompilerParams(vmem_limit_bytes=40 * 1024 * 1024),
        cost_estimate=pl.CostEstimate(
            flops=4 * tok * width * (width + c_out), bytes_accessed=2 * width * width, transcendentals=0
        ),
        name="finish",
    )(half_weight, ra, rb, rc, hidden_in, gate, mod, out_bias, final_weight, final_bias, out_weight)


def ring_stage(x, axis, size, move, combine):
    pairs = [[(i, move(i, k)) for i in range(size)] for k in (1, 2, 3)]
    others = [lax.ppermute(x, axis, p) for p in pairs]
    return combine(combine(x, others[0]), combine(others[1], others[2]))


def local(
    latent, hidden_in, img_query, img_key, img_value, txt_key, txt_value, text_len, head_slot,
    out_weight, out_bias, attn_gate, final_mod, final_weight, final_bias, timesteps, guidance,
):
    shards = lax.axis_size("seq")
    position = lax.axis_index("seq")
    head_count = head_slot.shape[0]
    model_width = out_weight.shape[0]
    tok, txt = img_query.shape[2], txt_key.shape[2]
    image_rows = tok * shards
    per_shard = (head_count + shards - 1) // shards

    streams = (img_query, img_key, img_value, txt_key, txt_value)

    def swap(x):
        return lax.all_to_all(x, "seq", split_axis=0, concat_axis=0, tiled=True)

    lengths = text_len[0]
    length_c = jnp.where((position % 4) // 2 == 0, lengths[0], lengths[1])

    in_a = swap(pack_pairs(0, *streams, shards))
    in_b = swap(pack_pairs(1, *streams, shards))
    in_c = swap(pack_single(*streams, shards))
    out_a, top_a = attend(in_a, lengths[0:1], tok, txt, False)
    back_a = swap(out_a)
    out_b, top_b = attend(in_b, lengths[1:2], tok, txt, False)
    back_b = swap(out_b)
    out_c, top_c = attend(in_c, length_c[None], tok, txt, True)
    back_c = swap(out_c)

    half_weight = jnp.where(lax.axis_index("cfg") == 0, guidance, 1.0 - guidance)
    pred, squares = finish(
        half_weight, back_a, back_b, back_c, hidden_in, attn_gate, final_mod,
        out_bias[None], final_weight, final_bias[None], out_weight,
    )
    velocity = pred + lax.ppermute(pred, "cfg", [(0, 1), (1, 0)])
    step_size = (sigma_of(timesteps - 1) - sigma_of(timesteps))[:, None, None]
    latent_next = latent + step_size * velocity

    lane = jnp.arange(LANES, dtype=jnp.int32)
    pair_top = jnp.maximum(top_a[0:2, 0], top_b[0:2, 0])
    single_top = jnp.maximum(top_c[0, 0], top_c[1, 0])
    single_head = 2 * shards + 2 * (position // 4) + position % 2
    table = jnp.full((LANES,), -jnp.inf, f32)
    table = jnp.where(lane == 2 * position, pair_top[0], table)
    table = jnp.where(lane == 2 * position + 1, pair_top[1], table)
    table = jnp.where((lane == single_head) & (single_head < head_count), single_top, table)
    table = jnp.maximum(table, lax.ppermute(table, "cfg", [(0, 1), (1, 0)]))
    table = ring_stage(table, "req", 4, lambda i, k: (i + k) % 4, jnp.maximum)

    small = jnp.concatenate([table[: LANES - 2], squares[0:2, 0]])

    def combine(a, b):
        return jnp.where(lane < LANES - 2, jnp.maximum(a, b), a + b)

    small = ring_stage(small, "seq", shards, lambda i, k: i // 4 * 4 + (i + k) % 4, combine)
    small = ring_stage(small, "seq", shards, lambda i, k: (i + 4 * k) % shards, combine)
    hidden_norms = jnp.sqrt(small[LANES - 2 :] / (image_rows * model_width))[None, :]

    own_slots = position * per_shard + jnp.arange(per_shard, dtype=jnp.int32)
    match = head_slot[None, :] == own_slots[:, None]
    best = jnp.max(jnp.where(match, small[None, :head_count], -jnp.inf), axis=1)
    max_logits = jnp.where(jnp.any(match, axis=1), best, 0.0)
    return (velocity, latent_next, hidden_norms, max_logits)


def solution(mesh):
    in_specs = (
        P("req", "seq", None),
        P("cfg", "req", "seq", None),
        P("cfg", "req", "seq", None),
        P("cfg", "req", "seq", None),
        P("cfg", "req", "seq", None),
        P("cfg", "req", "seq", None),
        P("cfg", "req", "seq", None),
        P("cfg", "req"),
        P(),
        P(),
        P(),
        P("cfg", "req", None),
        P("cfg", "req", None, None),
        P(),
        P(),
        P("req"),
        P("req"),
    )
    out_specs = (P("req", "seq", None), P("req", "seq", None), P("cfg", "req"), P("seq"))
    return jax.shard_map(local, mesh=mesh, in_specs=in_specs, out_specs=out_specs, check_vma=False)
```

```python
import functools
import math

import jax
import jax.numpy as jnp
from jax import lax
from jax.experimental import pallas as pl
from jax.experimental.pallas import tpu as pltpu
from jax.sharding import PartitionSpec as P

STEPS = 28
LANES = 128
QT = 256
bf16 = jnp.bfloat16
f32 = jnp.float32


def sigma_of(step_idx):
    fraction = step_idx.astype(f32) / STEPS
    return 3.0 * fraction / (1.0 + 2.0 * fraction)


def text_rows(ref, r, cols):
    return ref[0, :, :, cols].astype(f32)[:, r, :].astype(bf16)


def pack_pairs_kernel(r, q_ref, k_ref, v_ref, tk_ref, tv_ref, out_ref):
    tok = q_ref.shape[2]
    txt = tk_ref.shape[1]
    for i in range(out_ref.shape[0]):
        cols = slice(i * LANES, (i + 1) * LANES)
        out_ref[i, 0:tok, :] = q_ref[0, 0, :, cols]
        out_ref[i, tok : 2 * tok, :] = k_ref[0, 0, :, cols]
        out_ref[i, 2 * tok : 3 * tok, :] = v_ref[0, 0, :, cols]
        out_ref[i, 3 * tok : 3 * tok + txt, :] = text_rows(tk_ref, r, cols)
        out_ref[i, 3 * tok + txt : 3 * tok + 2 * txt, :] = text_rows(tv_ref, r, cols)


def pack_pairs(r, q, k, v, tk, tv, shards):
    tok, txt = q.shape[2], tk.shape[1]
    rows = 3 * tok + 2 * txt
    per = 4
    img = pl.BlockSpec((1, 1, tok, per * LANES), lambda j: (0, r, 0, j))
    text = pl.BlockSpec((1, txt, 2, per * LANES), lambda j: (0, 0, 0, j))
    return pl.pallas_call(
        functools.partial(pack_pairs_kernel, r),
        grid=(shards // per,),
        in_specs=[img, img, img, text, text],
        out_specs=pl.BlockSpec((per, rows, LANES), lambda j: (j, 0, 0)),
        out_shape=jax.ShapeDtypeStruct((shards, rows, LANES), bf16),
        cost_estimate=pl.CostEstimate(flops=0, bytes_accessed=4 * shards * rows * LANES, transcendentals=0),
        name="pack_pairs",
    )(q, k, v, tk, tv)


def pack_single_kernel(n_pairs, q_ref, k_ref, v_ref, tk_ref, tv_ref, out_ref):
    j = pl.program_id(0)
    tok = q_ref.shape[2]
    txt = tk_ref.shape[1]
    half = tok // 2
    hd = LANES // 2

    @pl.when(j < n_pairs)
    def _():
        for r in range(2):
            for h in range(2):
                d = 2 * r + h
                for n, ref in enumerate((q_ref, k_ref, v_ref)):
                    x = ref[0, r]
                    top, low = x[:half], x[half:]
                    if h == 0:
                        folded = jnp.concatenate([top[:, :hd], low[:, :hd]], axis=1)
                    else:
                        folded = jnp.concatenate([top[:, hd:], low[:, hd:]], axis=1)
                    out_ref[d, n * half : (n + 1) * half, :] = folded
                for n, ref in enumerate((tk_ref, tv_ref)):
                    x = text_rows(ref, r, slice(0, LANES))[:, h * hd : (h + 1) * hd]
                    base = 3 * half + n * txt
                    out_ref[d, base : base + txt, :] = jnp.concatenate([x, x], axis=1)

    @pl.when(j >= n_pairs)
    def _():
        out_ref[...] = jnp.zeros_like(out_ref)


def pack_single(q, k, v, tk, tv, shards):
    tok, txt = q.shape[2], tk.shape[1]
    n_pairs = q.shape[3] // LANES - shards
    rows = 3 * (tok // 2) + 2 * txt
    last = n_pairs - 1
    img = pl.BlockSpec((1, 2, tok, LANES), lambda j: (0, 0, 0, shards + jnp.minimum(j, last)))
    text = pl.BlockSpec((1, txt, 2, LANES), lambda j: (0, 0, 0, shards + jnp.minimum(j, last)))
    return pl.pallas_call(
        functools.partial(pack_single_kernel, n_pairs),
        grid=(shards // 4,),
        in_specs=[img, img, img, text, text],
        out_specs=pl.BlockSpec((4, rows, LANES), lambda j: (j, 0, 0)),
        out_shape=jax.ShapeDtypeStruct((shards, rows, LANES), bf16),
        cost_estimate=pl.CostEstimate(flops=0, bytes_accessed=4 * shards * rows * LANES, transcendentals=0),
        name="pack_single",
    )(q, k, v, tk, tv)


def attend_kernel(which, carried, folded, tok, txt, len_ref, r_ref, *refs):
    c_ref = refs[0] if carried else None
    o_ref, top_ref, k2, vt, top = refs[-5:]
    shards = r_ref.shape[0]
    hd = LANES // 2
    rows = tok // 2 if folded else tok
    n_img = shards * tok
    slot = 16
    n_txt = shards * slot
    t = pl.program_id(0)
    length = len_ref[which]

    @pl.when(t == 0)
    def _prep():
        for s in range(shards):
            kb = r_ref[s, rows : 2 * rows, :]
            at = slice(s * rows, (s + 1) * rows)
            k2[at, 0:LANES] = kb
            k2[at, LANES:] = kb
            if folded:
                other = jnp.concatenate([kb[:, hd:], kb[:, :hd]], axis=1)
                at2 = slice(n_img // 2 + s * rows, n_img // 2 + (s + 1) * rows)
                k2[at2, 0:LANES] = other
                k2[at2, LANES:] = other
        step = LANES // rows
        for u in range(shards // step):
            vb = r_ref[u * step : (u + 1) * step, 2 * rows : 3 * rows, :].reshape(LANES, LANES)
            vb = vb.astype(f32).T.astype(bf16)
            at = slice(u * LANES, (u + 1) * LANES)
            vt[0, 0:hd, at] = vb[:hd]
            vt[1, 0:hd, at] = vb[hd:]
            if folded:
                at2 = slice(n_img // 2 + u * LANES, n_img // 2 + (u + 1) * LANES)
                vt[0, 0:hd, at2] = vb[hd:]
                vt[1, 0:hd, at2] = vb[:hd]
        tks, tvs = [], []
        pad = jnp.zeros((slot - txt, LANES), f32)
        for s in range(shards):
            tks += [r_ref[s, 3 * rows : 3 * rows + txt, :].astype(f32), pad]
            tvs += [r_ref[s, 3 * rows + txt : 3 * rows + 2 * txt, :].astype(f32), pad]
        tkx = jnp.concatenate(tks, axis=0)
        tvx = jnp.concatenate(tvs, axis=0)
        i = lax.broadcasted_iota(jnp.int32, (n_txt, LANES), 0)
        live = ((i % slot) < txt) & ((i // slot) * txt + (i % slot) < length)
        key0 = k2[0:16, 0:LANES].astype(f32)[0:1]
        tkx = jnp.where(live, tkx, jnp.broadcast_to(key0, (n_txt, LANES))).astype(bf16)
        k2[n_img:, 0:LANES] = tkx
        k2[n_img:, LANES:] = tkx
        tvx = jnp.where(live, tvx, 0.0)
        for u in range(n_txt // LANES):
            vb = tvx[u * LANES : (u + 1) * LANES].T.astype(bf16)
            at = slice(n_img + u * LANES, n_img + (u + 1) * LANES)
            vt[0, 0:hd, at] = vb[:hd]
            vt[1, 0:hd, at] = vb[hd:]
        c = lax.broadcasted_iota(jnp.int32, (slot, n_txt), 1)
        live_t = ((c % slot) < txt) & ((c // slot) * txt + (c % slot) < length)
        ones_t = jnp.where(live_t, 1.0, 0.0).astype(bf16)
        for h in range(2):
            vt[h, hd:, 0:n_img] = jnp.ones((slot, n_img), bf16)
            vt[h, hd:, n_img:] = ones_t
        top[...] = jnp.full(top.shape, -jnp.inf, f32)

    per = QT // rows
    q = r_ref[pl.ds(t * per, per), 0:rows, :].reshape(QT, LANES).astype(f32)
    q = q * (math.log2(math.e) / math.sqrt(hd))
    lane = lax.broadcasted_iota(jnp.int32, (QT, LANES), 1)
    outs = []
    for h in range(2):
        qh = jnp.where((lane >= hd) == (h == 1), q, 0.0)
        hi = qh.astype(bf16)
        lo = (qh - hi.astype(f32)).astype(bf16)
        q2 = jnp.concatenate([hi, lo], axis=1)
        s = lax.dot_general(k2[...], q2, (((1,), (1,)), ((), ())), preferred_element_type=f32)
        m = jnp.max(s, axis=0, keepdims=True)
        p = jnp.exp2(s - m).astype(bf16)
        o = jnp.dot(vt[h], p, preferred_element_type=f32)
        outs.append(o[:hd] / o[hd : hd + 1])
        top[h : h + 1, :] = jnp.maximum(top[h : h + 1, :], m)
    out = jnp.concatenate(outs, axis=0).T.astype(bf16)
    o_ref[:, 0:rows, :] = out.reshape(per, rows, LANES)
    if carried:
        o_ref[:, rows:, :] = c_ref[...]

    @pl.when(t == pl.num_programs(0) - 1)
    def _fin():
        best = jnp.max(top[...], axis=1, keepdims=True) * math.log(2.0)
        top_ref[...] = jnp.broadcast_to(best, top_ref.shape)


def attend(received, lengths, which, tok, txt, folded, carry=None):
    shards, total, _ = received.shape
    rows = tok // 2 if folded else tok
    n_keys = shards * (tok + 16)
    per = QT // rows
    heads = 1 if folded else 2
    extra = [] if carry is None else [carry]
    out_rows = rows + sum(x.shape[1] for x in extra)
    return pl.pallas_call(
        functools.partial(attend_kernel, which, carry is not None, folded, tok, txt),
        grid=(shards // per,),
        in_specs=[
            pl.BlockSpec(memory_space=pltpu.SMEM),
            pl.BlockSpec((shards, total, LANES), lambda t: (0, 0, 0)),
        ]
        + [pl.BlockSpec((per,) + x.shape[1:], lambda t: (t, 0, 0)) for x in extra],
        out_specs=[
            pl.BlockSpec((per, out_rows, LANES), lambda t: (t, 0, 0)),
            pl.BlockSpec((8, LANES), lambda t: (0, 0)),
        ],
        out_shape=[
            jax.ShapeDtypeStruct((shards, out_rows, LANES), bf16),
            jax.ShapeDtypeStruct((8, LANES), f32),
        ],
        scratch_shapes=[
            pltpu.VMEM((n_keys, 2 * LANES), bf16),
            pltpu.VMEM((2, LANES // 2 + 16, n_keys), bf16),
            pltpu.VMEM((8, QT), f32),
        ],
        compiler_params=pltpu.CompilerParams(vmem_limit_bytes=40 * 1024 * 1024),
        cost_estimate=pl.CostEstimate(
            flops=heads * 4 * shards * tok * n_keys * LANES,
            bytes_accessed=4 * shards * total * LANES,
            transcendentals=heads * shards * tok * n_keys,
        ),
        name="attend_single" if folded else "attend_pair",
    )(lengths, received, *extra)


def finish_kernel(
    n_pairs, half_ref, a_ref, b_ref, hid_ref, gate_ref, mod_ref, ob_ref, fw_ref, w_hbm,
    pred_ref, sq_ref, att, w, acc, sem,
):
    shards, tok, _ = b_ref.shape
    width = w.shape[0]
    hd = LANES // 2
    half = tok // 2
    edges = list(range(0, width, 4 * LANES)) + [width]
    copies = [
        pltpu.make_async_copy(w_hbm.at[lo:up, :], w.at[lo:up, :], sem.at[n])
        for n, (lo, up) in enumerate(zip(edges[:-1], edges[1:]))
    ]
    for copy in copies:
        copy.start()
    for d in range(shards):
        att[0:tok, d * LANES : (d + 1) * LANES] = a_ref[d, 0:tok]
        att[tok:, d * LANES : (d + 1) * LANES] = b_ref[d]
    for j in range(n_pairs):
        for r in range(2):
            x0 = a_ref[4 * j + 2 * r, tok:]
            x1 = a_ref[4 * j + 2 * r + 1, tok:]
            cols = slice((shards + j) * LANES, (shards + j + 1) * LANES)
            att[r * tok : r * tok + half, cols] = jnp.concatenate([x0[:, :hd], x1[:, :hd]], axis=1)
            att[r * tok + half : (r + 1) * tok, cols] = jnp.concatenate([x0[:, hd:], x1[:, hd:]], axis=1)
    for n, (lo, up) in enumerate(zip(edges[:-1], edges[1:])):
        copies[n].wait()
        part = jnp.dot(att[:, lo:up], w[lo:up, :], preferred_element_type=f32)
        if n == 0:
            acc[...] = part
        else:
            acc[...] += part

    step = 16
    for r in range(2):
        gate = gate_ref[0, r : r + 1, :]
        shift = mod_ref[0, r, 0:1, :]
        scale = 1.0 + mod_ref[0, r, 1:2, :]
        bias = ob_ref[...]

        def body(i, total):
            at = pl.ds(r * tok + i * step, step)
            hid = hid_ref[0, r, pl.ds(i * step, step), :].astype(f32) + gate * (acc[at, :] + bias)
            total = total + jnp.sum(hid * hid, axis=1, keepdims=True)
            mean = jnp.mean(hid, axis=1, keepdims=True)
            cen = hid - mean
            var = jnp.mean(cen * cen, axis=1, keepdims=True)
            att[at, :] = (cen / jnp.sqrt(var + 1e-6) * scale + shift).astype(bf16)
            return total

        total = lax.fori_loop(0, tok // step, body, jnp.zeros((step, 1), f32))
        sq_ref[r : r + 1, :] = jnp.broadcast_to(jnp.sum(total, axis=0, keepdims=True), (1, LANES))
        pred = lax.dot_general(
            fw_ref[...], att[r * tok : (r + 1) * tok, :], (((1,), (1,)), ((), ())), preferred_element_type=f32
        )
        pred_ref[r] = half_ref[r] * pred


def finish(half_weight, ra, rb, hidden_in, gate, mod, out_bias, final_weight, out_weight):
    shards, tok, _ = rb.shape
    width = out_weight.shape[0]
    c_out = final_weight.shape[0]
    n_pairs = width // LANES - shards
    vmem = pl.BlockSpec(memory_space=pltpu.VMEM)
    return pl.pallas_call(
        functools.partial(finish_kernel, n_pairs),
        in_specs=[pl.BlockSpec(memory_space=pltpu.SMEM)] + [vmem] * 7 + [pl.BlockSpec(memory_space=pl.ANY)],
        out_specs=[vmem, vmem],
        out_shape=[
            jax.ShapeDtypeStruct((2, c_out, tok), f32),
            jax.ShapeDtypeStruct((8, LANES), f32),
        ],
        scratch_shapes=[
            pltpu.VMEM((2 * tok, width), bf16),
            pltpu.VMEM((width, width), bf16),
            pltpu.VMEM((2 * tok, width), f32),
            pltpu.SemaphoreType.DMA((5,)),
        ],
        compiler_params=pltpu.CompilerParams(vmem_limit_bytes=40 * 1024 * 1024),
        cost_estimate=pl.CostEstimate(
            flops=4 * tok * width * (width + c_out), bytes_accessed=2 * width * width, transcendentals=0
        ),
        name="finish",
    )(half_weight, ra, rb, hidden_in, gate, mod, out_bias, final_weight, out_weight)


def ring_stage(x, axis, size, move, combine):
    pairs = [[(i, move(i, k)) for i in range(size)] for k in (1, 2, 3)]
    others = [lax.ppermute(x, axis, p) for p in pairs]
    return combine(combine(x, others[0]), combine(others[1], others[2]))


def local(
    latent, hidden_in, img_query, img_key, img_value, txt_key, txt_value, text_len, head_slot,
    out_weight, out_bias, attn_gate, final_mod, final_weight, final_bias, timesteps, guidance,
):
    shards = lax.axis_size("seq")
    position = lax.axis_index("seq")
    head_count = head_slot.shape[0]
    model_width = out_weight.shape[0]
    tok, txt = img_query.shape[2], txt_key.shape[2]
    image_rows = tok * shards
    per_shard = (head_count + shards - 1) // shards

    text = [x.transpose(0, 2, 1, 3) for x in (txt_key, txt_value)]
    streams = (img_query, img_key, img_value, *text)

    def swap(x):
        return lax.all_to_all(x, "seq", split_axis=0, concat_axis=0, tiled=True)

    length_c = jnp.where((position % 4) // 2 == 0, text_len[0, 0], text_len[0, 1])
    lengths = jnp.stack([text_len[0, 0], text_len[0, 1], length_c])
    half_weight = jnp.where(lax.axis_index("cfg") == 0, guidance, 1.0 - guidance)
    lengths, half_weight, first = lax.optimization_barrier(
        (lengths, half_weight, pack_single(*streams, shards))
    )

    in_c = swap(first)
    in_a = swap(pack_pairs(0, *streams, shards))
    out_c, top_c = attend(in_c, lengths, 2, tok, txt, True)
    second, out_c = lax.optimization_barrier((pack_pairs(1, *streams, shards), out_c))
    in_b = swap(second)
    out_a, top_a = attend(in_a, lengths, 0, tok, txt, False, out_c)
    back_a = swap(out_a)
    out_b, top_b = attend(in_b, lengths, 1, tok, txt, False)
    back_b = swap(out_b)

    pred, squares = finish(
        half_weight, back_a, back_b, hidden_in, attn_gate, final_mod,
        out_bias[None], final_weight.T, out_weight,
    )
    velocity = pred + lax.ppermute(pred, "cfg", [(0, 1), (1, 0)]) + final_bias[None, :, None]
    step_size = (sigma_of(timesteps - 1) - sigma_of(timesteps))[:, None, None]
    latent_next = latent.transpose(0, 2, 1) + step_size * velocity
    velocity, latent_next = velocity.transpose(0, 2, 1), latent_next.transpose(0, 2, 1)

    lane = jnp.arange(LANES, dtype=jnp.int32)
    pair_top = jnp.maximum(top_a[0:2, 0], top_b[0:2, 0])
    single_top = jnp.maximum(top_c[0, 0], top_c[1, 0])
    single_head = 2 * shards + 2 * (position // 4) + position % 2
    table = jnp.full((LANES,), -jnp.inf, f32)
    table = jnp.where(lane == 2 * position, pair_top[0], table)
    table = jnp.where(lane == 2 * position + 1, pair_top[1], table)
    table = jnp.where((lane == single_head) & (single_head < head_count), single_top, table)
    table = jnp.maximum(table, lax.ppermute(table, "cfg", [(0, 1), (1, 0)]))
    table = ring_stage(table, "req", 4, lambda i, k: (i + k) % 4, jnp.maximum)

    small = jnp.concatenate([table[: LANES - 2], squares[0:2, 0]])

    def combine(a, b):
        return jnp.where(lane < LANES - 2, jnp.maximum(a, b), a + b)

    small = ring_stage(small, "seq", shards, lambda i, k: i // 4 * 4 + (i + k) % 4, combine)
    small = ring_stage(small, "seq", shards, lambda i, k: (i + 4 * k) % shards, combine)
    hidden_norms = jnp.sqrt(small[LANES - 2 :] / (image_rows * model_width))[None, :]

    own_slots = position * per_shard + jnp.arange(per_shard, dtype=jnp.int32)
    match = head_slot[None, :] == own_slots[:, None]
    best = jnp.max(jnp.where(match, small[None, :head_count], -jnp.inf), axis=1)
    max_logits = jnp.where(jnp.any(match, axis=1), best, 0.0)
    return (velocity, latent_next, hidden_norms, max_logits)


def solution(mesh):
    in_specs = (
        P("req", "seq", None),
        P("cfg", "req", "seq", None),
        P("cfg", "req", "seq", None),
        P("cfg", "req", "seq", None),
        P("cfg", "req", "seq", None),
        P("cfg", "req", "seq", None),
        P("cfg", "req", "seq", None),
        P("cfg", "req"),
        P(),
        P(),
        P(),
        P("cfg", "req", None),
        P("cfg", "req", None, None),
        P(),
        P(),
        P("req"),
        P("req"),
    )
    out_specs = (P("req", "seq", None), P("req", "seq", None), P("cfg", "req"), P("seq"))
    return jax.shard_map(local, mesh=mesh, in_specs=in_specs, out_specs=out_specs, check_vma=False)
```

```python
import functools
import math

import jax
import jax.numpy as jnp
from jax import lax
from jax.experimental import pallas as pl
from jax.experimental.pallas import tpu as pltpu
from jax.sharding import PartitionSpec as P

STEPS = 28
LANES = 128
QT = 512
TILE = 256
CHUNK = 256
bf16 = jnp.bfloat16
f32 = jnp.float32


def sigma_of(step_idx):
    fraction = step_idx.astype(f32) / STEPS
    return 3.0 * fraction / (1.0 + 2.0 * fraction)


def text_rows(ref, r, cols):
    return ref[0, :, :, cols].astype(f32)[:, r, :].astype(bf16)


def pack_pairs_kernel(r, q_ref, k_ref, v_ref, tk_ref, tv_ref, out_ref):
    tok = q_ref.shape[2]
    txt = tk_ref.shape[1]
    for i in range(out_ref.shape[0]):
        cols = slice(i * LANES, (i + 1) * LANES)
        out_ref[i, 0:tok, :] = q_ref[0, 0, :, cols]
        out_ref[i, tok : 2 * tok, :] = k_ref[0, 0, :, cols]
        out_ref[i, 2 * tok : 3 * tok, :] = v_ref[0, 0, :, cols]
        out_ref[i, 3 * tok : 3 * tok + txt, :] = text_rows(tk_ref, r, cols)
        out_ref[i, 3 * tok + txt : 3 * tok + 2 * txt, :] = text_rows(tv_ref, r, cols)


def pack_pairs(r, q, k, v, tk, tv, shards):
    tok, txt = q.shape[2], tk.shape[1]
    rows = 3 * tok + 2 * txt
    per = 4
    img = pl.BlockSpec((1, 1, tok, per * LANES), lambda j: (0, r, 0, j))
    text = pl.BlockSpec((1, txt, 2, per * LANES), lambda j: (0, 0, 0, j))
    return pl.pallas_call(
        functools.partial(pack_pairs_kernel, r),
        grid=(shards // per,),
        in_specs=[img, img, img, text, text],
        out_specs=pl.BlockSpec((per, rows, LANES), lambda j: (j, 0, 0)),
        out_shape=jax.ShapeDtypeStruct((shards, rows, LANES), bf16),
        cost_estimate=pl.CostEstimate(flops=0, bytes_accessed=4 * shards * rows * LANES, transcendentals=0),
        name="pack_pairs",
    )(q, k, v, tk, tv)


def pack_single_kernel(n_pairs, q_ref, k_ref, v_ref, tk_ref, tv_ref, out_ref):
    j = pl.program_id(0)
    tok = q_ref.shape[2]
    txt = tk_ref.shape[1]
    half = tok // 2
    hd = LANES // 2

    @pl.when(j < n_pairs)
    def _():
        for r in range(2):
            for h in range(2):
                d = 2 * r + h
                for n, ref in enumerate((q_ref, k_ref, v_ref)):
                    x = ref[0, r]
                    top, low = x[:half], x[half:]
                    if h == 0:
                        folded = jnp.concatenate([top[:, :hd], low[:, :hd]], axis=1)
                    else:
                        folded = jnp.concatenate([top[:, hd:], low[:, hd:]], axis=1)
                    out_ref[d, n * half : (n + 1) * half, :] = folded
                for n, ref in enumerate((tk_ref, tv_ref)):
                    x = text_rows(ref, r, slice(0, LANES))[:, h * hd : (h + 1) * hd]
                    base = 3 * half + n * txt
                    out_ref[d, base : base + txt, :] = jnp.concatenate([x, x], axis=1)

    @pl.when(j >= n_pairs)
    def _():
        out_ref[...] = jnp.zeros_like(out_ref)


def pack_single(q, k, v, tk, tv, shards):
    tok, txt = q.shape[2], tk.shape[1]
    n_pairs = q.shape[3] // LANES - shards
    rows = 3 * (tok // 2) + 2 * txt
    last = n_pairs - 1
    img = pl.BlockSpec((1, 2, tok, LANES), lambda j: (0, 0, 0, shards + jnp.minimum(j, last)))
    text = pl.BlockSpec((1, txt, 2, LANES), lambda j: (0, 0, 0, shards + jnp.minimum(j, last)))
    return pl.pallas_call(
        functools.partial(pack_single_kernel, n_pairs),
        grid=(shards // 4,),
        in_specs=[img, img, img, text, text],
        out_specs=pl.BlockSpec((4, rows, LANES), lambda j: (j, 0, 0)),
        out_shape=jax.ShapeDtypeStruct((shards, rows, LANES), bf16),
        cost_estimate=pl.CostEstimate(flops=0, bytes_accessed=4 * shards * rows * LANES, transcendentals=0),
        name="pack_single",
    )(q, k, v, tk, tv)


def attend_kernel(which, carried, folded, tok, txt, len_ref, r_ref, *refs):
    c_ref = refs[0] if carried else None
    o_ref, top_ref, k2, vt, top, sbuf = refs[-6:]
    shards = r_ref.shape[0]
    hd = LANES // 2
    rows = tok // 2 if folded else tok
    n_img = shards * tok
    slot = 16
    n_txt = shards * slot
    t = pl.program_id(0)
    request = which if which < 2 else (lax.axis_index("seq") % 4) // 2
    length = len_ref[0, request]

    @pl.when(t == 0)
    def _prep():
        for s in range(shards):
            kb = r_ref[s, rows : 2 * rows, :]
            at = slice(s * rows, (s + 1) * rows)
            k2[at, 0:LANES] = kb
            k2[at, LANES:] = kb
            if folded:
                other = jnp.concatenate([kb[:, hd:], kb[:, :hd]], axis=1)
                at2 = slice(n_img // 2 + s * rows, n_img // 2 + (s + 1) * rows)
                k2[at2, 0:LANES] = other
                k2[at2, LANES:] = other
        step = LANES // rows
        for u in range(shards // step):
            vb = r_ref[u * step : (u + 1) * step, 2 * rows : 3 * rows, :].reshape(LANES, LANES)
            vb = vb.astype(f32).T.astype(bf16)
            at = slice(u * LANES, (u + 1) * LANES)
            vt[0, 0:hd, at] = vb[:hd]
            vt[1, 0:hd, at] = vb[hd:]
            if folded:
                at2 = slice(n_img // 2 + u * LANES, n_img // 2 + (u + 1) * LANES)
                vt[0, 0:hd, at2] = vb[hd:]
                vt[1, 0:hd, at2] = vb[:hd]
        tks, tvs = [], []
        pad = jnp.zeros((slot - txt, LANES), f32)
        for s in range(shards):
            tks += [r_ref[s, 3 * rows : 3 * rows + txt, :].astype(f32), pad]
            tvs += [r_ref[s, 3 * rows + txt : 3 * rows + 2 * txt, :].astype(f32), pad]
        tkx = jnp.concatenate(tks, axis=0)
        tvx = jnp.concatenate(tvs, axis=0)
        i = lax.broadcasted_iota(jnp.int32, (n_txt, LANES), 0)
        live = ((i % slot) < txt) & ((i // slot) * txt + (i % slot) < length)
        key0 = k2[0:16, 0:LANES].astype(f32)[0:1]
        tkx = jnp.where(live, tkx, jnp.broadcast_to(key0, (n_txt, LANES))).astype(bf16)
        k2[n_img:, 0:LANES] = tkx
        k2[n_img:, LANES:] = tkx
        tvx = jnp.where(live, tvx, 0.0)
        for u in range(n_txt // LANES):
            vb = tvx[u * LANES : (u + 1) * LANES].T.astype(bf16)
            at = slice(n_img + u * LANES, n_img + (u + 1) * LANES)
            vt[0, 0:hd, at] = vb[:hd]
            vt[1, 0:hd, at] = vb[hd:]
        c = lax.broadcasted_iota(jnp.int32, (slot, n_txt), 1)
        live_t = ((c % slot) < txt) & ((c // slot) * txt + (c % slot) < length)
        ones_t = jnp.where(live_t, 1.0, 0.0).astype(bf16)
        for h in range(2):
            vt[h, hd:, 0:n_img] = jnp.ones((slot, n_img), bf16)
            vt[h, hd:, n_img:] = ones_t
        top[...] = jnp.full(top.shape, -jnp.inf, f32)

    per = QT // rows
    q = r_ref[pl.ds(t * per, per), 0:rows, :].reshape(QT, LANES).astype(f32)
    q = q * (math.log2(math.e) / math.sqrt(hd))
    lane = lax.broadcasted_iota(jnp.int32, (QT, LANES), 1)
    queries = []
    for h in range(2):
        qh = jnp.where((lane >= hd) == (h == 1), q, 0.0)
        hi = qh.astype(bf16)
        lo = (qh - hi.astype(f32)).astype(bf16)
        queries.append(jnp.concatenate([hi, lo], axis=1))
    units = [(i, h) for i in range(QT // TILE) for h in range(2)]
    n_keys = k2.shape[0]
    outs = {}
    m = None
    for u in range(len(units) + 1):
        if u < len(units):
            i, h = units[u]
            qu = queries[h][i * TILE : (i + 1) * TILE]
        part, acc = None, None
        for lo in range(0, n_keys, CHUNK):
            at = slice(lo, lo + CHUNK)
            if u < len(units):
                s = lax.dot_general(k2[at, :], qu, (((1,), (1,)), ((), ())), preferred_element_type=f32)
                sbuf[u % 2, at, :] = s
                top8 = jnp.max(s.reshape(CHUNK // 8, 8, TILE), axis=0)
                part = top8 if part is None else jnp.maximum(part, top8)
            if u > 0:
                p = jnp.exp2(sbuf[(u - 1) % 2, at, :] - m).astype(bf16)
                o = jnp.dot(vt[units[u - 1][1], :, at], p, preferred_element_type=f32)
                acc = o if acc is None else acc + o
        if u > 0:
            outs[units[u - 1]] = acc[:hd] / acc[hd : hd + 1]
        if u < len(units):
            m = jnp.max(part, axis=0, keepdims=True)
            top[h : h + 1, :] = jnp.maximum(top[h : h + 1, :], m)
    out = jnp.concatenate(
        [jnp.concatenate([outs[i, h] for h in range(2)], axis=0).T.astype(bf16) for i in range(QT // TILE)], axis=0
    )
    o_ref[:, 0:rows, :] = out.reshape(per, rows, LANES)
    if carried:
        o_ref[:, rows:, :] = c_ref[...]

    @pl.when(t == pl.num_programs(0) - 1)
    def _fin():
        best = jnp.max(top[...], axis=1, keepdims=True) * math.log(2.0)
        top_ref[...] = jnp.broadcast_to(best, top_ref.shape)


def attend(received, lengths, which, tok, txt, folded, carry=None):
    shards, total, _ = received.shape
    rows = tok // 2 if folded else tok
    n_keys = shards * (tok + 16)
    per = QT // rows
    heads = 1 if folded else 2
    extra = [] if carry is None else [carry]
    out_rows = rows + sum(x.shape[1] for x in extra)
    return pl.pallas_call(
        functools.partial(attend_kernel, which, carry is not None, folded, tok, txt),
        grid=(shards // per,),
        in_specs=[
            pl.BlockSpec(memory_space=pltpu.SMEM),
            pl.BlockSpec((shards, total, LANES), lambda t: (0, 0, 0)),
        ]
        + [pl.BlockSpec((per,) + x.shape[1:], lambda t: (t, 0, 0)) for x in extra],
        out_specs=[
            pl.BlockSpec((per, out_rows, LANES), lambda t: (t, 0, 0)),
            pl.BlockSpec((8, LANES), lambda t: (0, 0)),
        ],
        out_shape=[
            jax.ShapeDtypeStruct((shards, out_rows, LANES), bf16),
            jax.ShapeDtypeStruct((8, LANES), f32),
        ],
        scratch_shapes=[
            pltpu.VMEM((n_keys, 2 * LANES), bf16),
            pltpu.VMEM((2, LANES // 2 + 16, n_keys), bf16),
            pltpu.VMEM((8, TILE), f32),
            pltpu.VMEM((2, n_keys, TILE), f32),
        ],
        compiler_params=pltpu.CompilerParams(vmem_limit_bytes=24 * 1024 * 1024),
        cost_estimate=pl.CostEstimate(
            flops=heads * 4 * shards * tok * n_keys * LANES,
            bytes_accessed=4 * shards * total * LANES,
            transcendentals=heads * shards * tok * n_keys,
        ),
        name="attend_single" if folded else "attend_pair",
    )(lengths, received, *extra)


def finish_kernel(
    n_pairs, guide_ref, a_ref, b_ref, hid_ref, gate_ref, mod_ref, ob_ref, fw_ref, w_hbm,
    pred_ref, sq_ref, att, w, acc, sem,
):
    shards, tok, _ = b_ref.shape
    width = w.shape[0]
    hd = LANES // 2
    half = tok // 2
    edges = list(range(0, width, 4 * LANES)) + [width]
    copies = [
        pltpu.make_async_copy(w_hbm.at[lo:up, :], w.at[lo:up, :], sem.at[n])
        for n, (lo, up) in enumerate(zip(edges[:-1], edges[1:]))
    ]
    for copy in copies:
        copy.start()
    for d in range(shards):
        att[0:tok, d * LANES : (d + 1) * LANES] = a_ref[d, 0:tok]
        att[tok:, d * LANES : (d + 1) * LANES] = b_ref[d]
    for j in range(n_pairs):
        for r in range(2):
            x0 = a_ref[4 * j + 2 * r, tok:]
            x1 = a_ref[4 * j + 2 * r + 1, tok:]
            cols = slice((shards + j) * LANES, (shards + j + 1) * LANES)
            att[r * tok : r * tok + half, cols] = jnp.concatenate([x0[:, :hd], x1[:, :hd]], axis=1)
            att[r * tok + half : (r + 1) * tok, cols] = jnp.concatenate([x0[:, hd:], x1[:, hd:]], axis=1)
    for n, (lo, up) in enumerate(zip(edges[:-1], edges[1:])):
        copies[n].wait()
        part = jnp.dot(att[:, lo:up], w[lo:up, :], preferred_element_type=f32)
        if n == 0:
            acc[...] = part
        else:
            acc[...] += part

    step = 16
    for r in range(2):
        gate = gate_ref[0, r : r + 1, :]
        shift = mod_ref[0, r, 0:1, :]
        scale = 1.0 + mod_ref[0, r, 1:2, :]
        bias = ob_ref[...]

        def body(i, total):
            at = pl.ds(r * tok + i * step, step)
            hid = hid_ref[0, r, pl.ds(i * step, step), :].astype(f32) + gate * (acc[at, :] + bias)
            total = total + jnp.sum(hid * hid, axis=1, keepdims=True)
            mean = jnp.mean(hid, axis=1, keepdims=True)
            cen = hid - mean
            var = jnp.mean(cen * cen, axis=1, keepdims=True)
            att[at, :] = (cen / jnp.sqrt(var + 1e-6) * scale + shift).astype(bf16)
            return total

        total = lax.fori_loop(0, tok // step, body, jnp.zeros((step, 1), f32))
        sq_ref[r : r + 1, :] = jnp.broadcast_to(jnp.sum(total, axis=0, keepdims=True), (1, LANES))
        pred = lax.dot_general(
            fw_ref[...], att[r * tok : (r + 1) * tok, :], (((1,), (1,)), ((), ())), preferred_element_type=f32
        )
        cond = lax.axis_index("cfg") == 0
        pred_ref[r] = jnp.where(cond, guide_ref[r], 1.0 - guide_ref[r]) * pred


def finish(guidance, ra, rb, hidden_in, gate, mod, out_bias, final_weight, out_weight):
    shards, tok, _ = rb.shape
    width = out_weight.shape[0]
    c_out = final_weight.shape[0]
    n_pairs = width // LANES - shards
    vmem = pl.BlockSpec(memory_space=pltpu.VMEM)
    return pl.pallas_call(
        functools.partial(finish_kernel, n_pairs),
        in_specs=[pl.BlockSpec(memory_space=pltpu.SMEM)] + [vmem] * 7 + [pl.BlockSpec(memory_space=pl.ANY)],
        out_specs=[vmem, vmem],
        out_shape=[
            jax.ShapeDtypeStruct((2, c_out, tok), f32),
            jax.ShapeDtypeStruct((8, LANES), f32),
        ],
        scratch_shapes=[
            pltpu.VMEM((2 * tok, width), bf16),
            pltpu.VMEM((width, width), bf16),
            pltpu.VMEM((2 * tok, width), f32),
            pltpu.SemaphoreType.DMA((5,)),
        ],
        compiler_params=pltpu.CompilerParams(vmem_limit_bytes=40 * 1024 * 1024),
        cost_estimate=pl.CostEstimate(
            flops=4 * tok * width * (width + c_out), bytes_accessed=2 * width * width, transcendentals=0
        ),
        name="finish",
    )(guidance, ra, rb, hidden_in, gate, mod, out_bias, final_weight, out_weight)


def ring_stage(x, axis, size, move, combine):
    pairs = [[(i, move(i, k)) for i in range(size)] for k in (1, 2, 3)]
    others = [lax.ppermute(x, axis, p) for p in pairs]
    return combine(combine(x, others[0]), combine(others[1], others[2]))


def local(
    latent, hidden_in, img_query, img_key, img_value, txt_key, txt_value, text_len, head_slot,
    out_weight, out_bias, attn_gate, final_mod, final_weight, final_bias, timesteps, guidance,
):
    shards = lax.axis_size("seq")
    position = lax.axis_index("seq")
    head_count = head_slot.shape[0]
    model_width = out_weight.shape[0]
    tok, txt = img_query.shape[2], txt_key.shape[2]
    image_rows = tok * shards
    per_shard = (head_count + shards - 1) // shards

    text = [x.transpose(0, 2, 1, 3) for x in (txt_key, txt_value)]
    streams = (img_query, img_key, img_value, *text)

    def swap(x):
        return lax.all_to_all(x, "seq", split_axis=0, concat_axis=0, tiled=True)

    in_c = swap(pack_single(*streams, shards))
    in_a = swap(pack_pairs(0, *streams, shards))
    out_c, top_c = attend(in_c, text_len, 2, tok, txt, True)
    second, out_c = lax.optimization_barrier((pack_pairs(1, *streams, shards), out_c))
    in_b = swap(second)
    out_a, top_a = attend(in_a, text_len, 0, tok, txt, False, out_c)
    back_a = swap(out_a)
    out_b, top_b = attend(in_b, text_len, 1, tok, txt, False)
    back_b = swap(out_b)

    pred, squares = finish(
        guidance, back_a, back_b, hidden_in, attn_gate, final_mod,
        out_bias[None], final_weight.T, out_weight,
    )
    velocity = pred + lax.ppermute(pred, "cfg", [(0, 1), (1, 0)]) + final_bias[None, :, None]
    step_size = (sigma_of(timesteps - 1) - sigma_of(timesteps))[:, None, None]
    latent_next = latent.transpose(0, 2, 1) + step_size * velocity
    velocity, latent_next = velocity.transpose(0, 2, 1), latent_next.transpose(0, 2, 1)

    lane = jnp.arange(LANES, dtype=jnp.int32)
    pair_top = jnp.maximum(top_a[0:2, 0], top_b[0:2, 0])
    single_top = jnp.maximum(top_c[0, 0], top_c[1, 0])
    single_head = 2 * shards + 2 * (position // 4) + position % 2
    table = jnp.full((LANES,), -jnp.inf, f32)
    table = jnp.where(lane == 2 * position, pair_top[0], table)
    table = jnp.where(lane == 2 * position + 1, pair_top[1], table)
    table = jnp.where((lane == single_head) & (single_head < head_count), single_top, table)
    table = jnp.maximum(table, lax.ppermute(table, "cfg", [(0, 1), (1, 0)]))
    table = ring_stage(table, "req", 4, lambda i, k: (i + k) % 4, jnp.maximum)

    small = jnp.concatenate([table[: LANES - 2], squares[0:2, 0]])

    def combine(a, b):
        return jnp.where(lane < LANES - 2, jnp.maximum(a, b), a + b)

    small = ring_stage(small, "seq", shards, lambda i, k: i // 4 * 4 + (i + k) % 4, combine)
    small = ring_stage(small, "seq", shards, lambda i, k: (i + 4 * k) % shards, combine)
    hidden_norms = jnp.sqrt(small[LANES - 2 :] / (image_rows * model_width))[None, :]

    own_slots = position * per_shard + jnp.arange(per_shard, dtype=jnp.int32)
    match = head_slot[None, :] == own_slots[:, None]
    best = jnp.max(jnp.where(match, small[None, :head_count], -jnp.inf), axis=1)
    max_logits = jnp.where(jnp.any(match, axis=1), best, 0.0)
    return (velocity, latent_next, hidden_norms, max_logits)


def solution(mesh):
    in_specs = (
        P("req", "seq", None),
        P("cfg", "req", "seq", None),
        P("cfg", "req", "seq", None),
        P("cfg", "req", "seq", None),
        P("cfg", "req", "seq", None),
        P("cfg", "req", "seq", None),
        P("cfg", "req", "seq", None),
        P("cfg", "req"),
        P(),
        P(),
        P(),
        P("cfg", "req", None),
        P("cfg", "req", None, None),
        P(),
        P(),
        P("req"),
        P("req"),
    )
    out_specs = (P("req", "seq", None), P("req", "seq", None), P("cfg", "req"), P("seq"))
    return jax.shard_map(local, mesh=mesh, in_specs=in_specs, out_specs=out_specs, check_vma=False)
```

```python
import functools
import math

import jax
import jax.numpy as jnp
from jax import lax
from jax.experimental import pallas as pl
from jax.experimental.pallas import tpu as pltpu
from jax.sharding import PartitionSpec as P

STEPS = 28
LANES = 128
QT = 512
TILE = 256
CHUNK = 256
bf16 = jnp.bfloat16
f32 = jnp.float32


def sigma_of(step_idx):
    fraction = step_idx.astype(f32) / STEPS
    return 3.0 * fraction / (1.0 + 2.0 * fraction)


def text_rows(ref, r, cols):
    return ref[0, :, :, cols].astype(f32)[:, r, :].astype(bf16)


def pack_pairs_kernel(r, q_ref, k_ref, v_ref, tk_ref, tv_ref, out_ref):
    tok = q_ref.shape[2]
    txt = tk_ref.shape[1]
    for i in range(out_ref.shape[0]):
        cols = slice(i * LANES, (i + 1) * LANES)
        out_ref[i, 0:tok, :] = q_ref[0, 0, :, cols]
        out_ref[i, tok : 2 * tok, :] = k_ref[0, 0, :, cols]
        out_ref[i, 2 * tok : 3 * tok, :] = v_ref[0, 0, :, cols]
        out_ref[i, 3 * tok : 3 * tok + txt, :] = text_rows(tk_ref, r, cols)
        out_ref[i, 3 * tok + txt : 3 * tok + 2 * txt, :] = text_rows(tv_ref, r, cols)


def pack_pairs(r, q, k, v, tk, tv, shards):
    tok, txt = q.shape[2], tk.shape[1]
    rows = 3 * tok + 2 * txt
    per = 4
    img = pl.BlockSpec((1, 1, tok, per * LANES), lambda j: (0, r, 0, j))
    text = pl.BlockSpec((1, txt, 2, per * LANES), lambda j: (0, 0, 0, j))
    return pl.pallas_call(
        functools.partial(pack_pairs_kernel, r),
        grid=(shards // per,),
        in_specs=[img, img, img, text, text],
        out_specs=pl.BlockSpec((per, rows, LANES), lambda j: (j, 0, 0)),
        out_shape=jax.ShapeDtypeStruct((shards, rows, LANES), bf16),
        cost_estimate=pl.CostEstimate(flops=0, bytes_accessed=4 * shards * rows * LANES, transcendentals=0),
        name="pack_pairs",
    )(q, k, v, tk, tv)


def pack_single_kernel(n_pairs, q_ref, k_ref, v_ref, tk_ref, tv_ref, out_ref):
    j = pl.program_id(0)
    tok = q_ref.shape[2]
    txt = tk_ref.shape[1]
    half = tok // 2
    hd = LANES // 2

    @pl.when(j < n_pairs)
    def _():
        for r in range(2):
            for h in range(2):
                d = 2 * r + h
                for n, ref in enumerate((q_ref, k_ref, v_ref)):
                    x = ref[0, r]
                    top, low = x[:half], x[half:]
                    if h == 0:
                        folded = jnp.concatenate([top[:, :hd], low[:, :hd]], axis=1)
                    else:
                        folded = jnp.concatenate([top[:, hd:], low[:, hd:]], axis=1)
                    out_ref[d, n * half : (n + 1) * half, :] = folded
                for n, ref in enumerate((tk_ref, tv_ref)):
                    x = text_rows(ref, r, slice(0, LANES))[:, h * hd : (h + 1) * hd]
                    base = 3 * half + n * txt
                    out_ref[d, base : base + txt, :] = jnp.concatenate([x, x], axis=1)

    @pl.when(j >= n_pairs)
    def _():
        out_ref[...] = jnp.zeros_like(out_ref)


def pack_single(q, k, v, tk, tv, shards):
    tok, txt = q.shape[2], tk.shape[1]
    n_pairs = q.shape[3] // LANES - shards
    rows = 3 * (tok // 2) + 2 * txt
    last = n_pairs - 1
    img = pl.BlockSpec((1, 2, tok, LANES), lambda j: (0, 0, 0, shards + jnp.minimum(j, last)))
    text = pl.BlockSpec((1, txt, 2, LANES), lambda j: (0, 0, 0, shards + jnp.minimum(j, last)))
    return pl.pallas_call(
        functools.partial(pack_single_kernel, n_pairs),
        grid=(shards // 4,),
        in_specs=[img, img, img, text, text],
        out_specs=pl.BlockSpec((4, rows, LANES), lambda j: (j, 0, 0)),
        out_shape=jax.ShapeDtypeStruct((shards, rows, LANES), bf16),
        cost_estimate=pl.CostEstimate(flops=0, bytes_accessed=4 * shards * rows * LANES, transcendentals=0),
        name="pack_single",
    )(q, k, v, tk, tv)


def attend_kernel(which, carried, folded, tok, txt, len_ref, r_ref, *refs):
    c_ref = refs[0] if carried else None
    o_ref, top_ref, k2, vt, top, sbuf = refs[-6:]
    shards = r_ref.shape[0]
    hd = LANES // 2
    rows = tok // 2 if folded else tok
    n_img = shards * tok
    slot = 16
    n_txt = shards * slot
    t = pl.program_id(0)
    request = which if which < 2 else (lax.axis_index("seq") % 4) // 2
    length = len_ref[0, request]

    @pl.when(t == 0)
    def _prep():
        for s in range(shards):
            kb = r_ref[s, rows : 2 * rows, :]
            at = slice(s * rows, (s + 1) * rows)
            k2[at, 0:LANES] = kb
            k2[at, LANES:] = kb
            if folded:
                other = jnp.concatenate([kb[:, hd:], kb[:, :hd]], axis=1)
                at2 = slice(n_img // 2 + s * rows, n_img // 2 + (s + 1) * rows)
                k2[at2, 0:LANES] = other
                k2[at2, LANES:] = other
        step = LANES // rows
        for u in range(shards // step):
            vb = r_ref[u * step : (u + 1) * step, 2 * rows : 3 * rows, :].reshape(LANES, LANES)
            vb = vb.astype(f32).T.astype(bf16)
            at = slice(u * LANES, (u + 1) * LANES)
            vt[0, 0:hd, at] = vb[:hd]
            vt[1, 0:hd, at] = vb[hd:]
            if folded:
                at2 = slice(n_img // 2 + u * LANES, n_img // 2 + (u + 1) * LANES)
                vt[0, 0:hd, at2] = vb[hd:]
                vt[1, 0:hd, at2] = vb[:hd]
        tks, tvs = [], []
        pad = jnp.zeros((slot - txt, LANES), f32)
        for s in range(shards):
            tks += [r_ref[s, 3 * rows : 3 * rows + txt, :].astype(f32), pad]
            tvs += [r_ref[s, 3 * rows + txt : 3 * rows + 2 * txt, :].astype(f32), pad]
        tkx = jnp.concatenate(tks, axis=0)
        tvx = jnp.concatenate(tvs, axis=0)
        i = lax.broadcasted_iota(jnp.int32, (n_txt, LANES), 0)
        live = ((i % slot) < txt) & ((i // slot) * txt + (i % slot) < length)
        key0 = k2[0:16, 0:LANES].astype(f32)[0:1]
        tkx = jnp.where(live, tkx, jnp.broadcast_to(key0, (n_txt, LANES))).astype(bf16)
        k2[n_img:, 0:LANES] = tkx
        k2[n_img:, LANES:] = tkx
        tvx = jnp.where(live, tvx, 0.0)
        for u in range(n_txt // LANES):
            vb = tvx[u * LANES : (u + 1) * LANES].T.astype(bf16)
            at = slice(n_img + u * LANES, n_img + (u + 1) * LANES)
            vt[0, 0:hd, at] = vb[:hd]
            vt[1, 0:hd, at] = vb[hd:]
        c = lax.broadcasted_iota(jnp.int32, (slot, n_txt), 1)
        live_t = ((c % slot) < txt) & ((c // slot) * txt + (c % slot) < length)
        ones_t = jnp.where(live_t, 1.0, 0.0).astype(bf16)
        for h in range(2):
            vt[h, hd:, 0:n_img] = jnp.ones((slot, n_img), bf16)
            vt[h, hd:, n_img:] = ones_t
        top[...] = jnp.full(top.shape, -jnp.inf, f32)

    per = QT // rows
    q = r_ref[pl.ds(t * per, per), 0:rows, :].reshape(QT, LANES).astype(f32)
    q = q * (math.log2(math.e) / math.sqrt(hd))
    lane = lax.broadcasted_iota(jnp.int32, (QT, LANES), 1)
    queries = []
    for h in range(2):
        qh = jnp.where((lane >= hd) == (h == 1), q, 0.0)
        hi = qh.astype(bf16)
        lo = (qh - hi.astype(f32)).astype(bf16)
        queries.append(jnp.concatenate([hi, lo], axis=1))
    units = [(i, h) for i in range(QT // TILE) for h in range(2)]
    n_keys = k2.shape[0]
    outs = {}
    m = None
    for u in range(len(units) + 1):
        if u < len(units):
            i, h = units[u]
            qu = queries[h][i * TILE : (i + 1) * TILE]
        part, acc = None, None
        for lo in range(0, n_keys, CHUNK):
            at = slice(lo, lo + CHUNK)
            if u < len(units):
                s = lax.dot_general(k2[at, :], qu, (((1,), (1,)), ((), ())), preferred_element_type=f32)
                sbuf[u % 2, at, :] = s
                top8 = jnp.max(s.reshape(CHUNK // 8, 8, TILE), axis=0)
                part = top8 if part is None else jnp.maximum(part, top8)
            if u > 0:
                p = jnp.exp2(sbuf[(u - 1) % 2, at, :] - m).astype(bf16)
                o = jnp.dot(vt[units[u - 1][1], :, at], p, preferred_element_type=f32)
                acc = o if acc is None else acc + o
        if u > 0:
            outs[units[u - 1]] = acc[:hd] / acc[hd : hd + 1]
        if u < len(units):
            m = jnp.max(part, axis=0, keepdims=True)
            top[h : h + 1, :] = jnp.maximum(top[h : h + 1, :], m)
    out = jnp.concatenate(
        [jnp.concatenate([outs[i, h] for h in range(2)], axis=0).T.astype(bf16) for i in range(QT // TILE)], axis=0
    )
    o_ref[:, 0:rows, :] = out.reshape(per, rows, LANES)
    if carried:
        o_ref[:, rows:, :] = c_ref[...]

    @pl.when(t == pl.num_programs(0) - 1)
    def _fin():
        best = jnp.max(top[...], axis=1, keepdims=True) * math.log(2.0)
        top_ref[...] = jnp.broadcast_to(best, top_ref.shape)


def attend(received, lengths, which, tok, txt, folded, carry=None):
    shards, total, _ = received.shape
    rows = tok // 2 if folded else tok
    n_keys = shards * (tok + 16)
    per = QT // rows
    heads = 1 if folded else 2
    extra = [] if carry is None else [carry]
    out_rows = rows + sum(x.shape[1] for x in extra)
    return pl.pallas_call(
        functools.partial(attend_kernel, which, carry is not None, folded, tok, txt),
        grid=(shards // per,),
        in_specs=[
            pl.BlockSpec(memory_space=pltpu.SMEM),
            pl.BlockSpec((shards, total, LANES), lambda t: (0, 0, 0)),
        ]
        + [pl.BlockSpec((per,) + x.shape[1:], lambda t: (t, 0, 0)) for x in extra],
        out_specs=[
            pl.BlockSpec((per, out_rows, LANES), lambda t: (t, 0, 0)),
            pl.BlockSpec((8, LANES), lambda t: (0, 0)),
        ],
        out_shape=[
            jax.ShapeDtypeStruct((shards, out_rows, LANES), bf16),
            jax.ShapeDtypeStruct((8, LANES), f32),
        ],
        scratch_shapes=[
            pltpu.VMEM((n_keys, 2 * LANES), bf16),
            pltpu.VMEM((2, LANES // 2 + 16, n_keys), bf16),
            pltpu.VMEM((8, TILE), f32),
            pltpu.VMEM((2, n_keys, TILE), f32),
        ],
        compiler_params=pltpu.CompilerParams(vmem_limit_bytes=24 * 1024 * 1024),
        cost_estimate=pl.CostEstimate(
            flops=heads * 4 * shards * tok * n_keys * LANES,
            bytes_accessed=4 * shards * total * LANES,
            transcendentals=heads * shards * tok * n_keys,
        ),
        name="attend_single" if folded else "attend_pair",
    )(lengths, received, *extra)


def finish_kernel(
    n_pairs, guide_ref, a_ref, b_ref, hid_ref, gate_ref, mod_ref, ob_ref, fw_ref, w_hbm,
    pred_ref, sq_ref, att, w, acc, sem,
):
    shards, tok, _ = b_ref.shape
    width = w.shape[0]
    hd = LANES // 2
    half = tok // 2
    edges = list(range(0, width, 4 * LANES)) + [width]
    copies = [
        pltpu.make_async_copy(w_hbm.at[lo:up, :], w.at[lo:up, :], sem.at[n])
        for n, (lo, up) in enumerate(zip(edges[:-1], edges[1:]))
    ]
    for copy in copies:
        copy.start()
    for d in range(shards):
        att[0:tok, d * LANES : (d + 1) * LANES] = a_ref[d, 0:tok]
        att[tok:, d * LANES : (d + 1) * LANES] = b_ref[d]
    for j in range(n_pairs):
        for r in range(2):
            x0 = a_ref[4 * j + 2 * r, tok:]
            x1 = a_ref[4 * j + 2 * r + 1, tok:]
            cols = slice((shards + j) * LANES, (shards + j + 1) * LANES)
            att[r * tok : r * tok + half, cols] = jnp.concatenate([x0[:, :hd], x1[:, :hd]], axis=1)
            att[r * tok + half : (r + 1) * tok, cols] = jnp.concatenate([x0[:, hd:], x1[:, hd:]], axis=1)
    for n, (lo, up) in enumerate(zip(edges[:-1], edges[1:])):
        copies[n].wait()
        part = jnp.dot(att[:, lo:up], w[lo:up, :], preferred_element_type=f32)
        if n == 0:
            acc[...] = part
        else:
            acc[...] += part

    step = 16
    for r in range(2):
        gate = gate_ref[0, r : r + 1, :]
        shift = mod_ref[0, r, 0:1, :]
        scale = 1.0 + mod_ref[0, r, 1:2, :]
        bias = ob_ref[...]

        def body(i, total):
            at = pl.ds(r * tok + i * step, step)
            hid = hid_ref[0, r, pl.ds(i * step, step), :].astype(f32) + gate * (acc[at, :] + bias)
            total = total + jnp.sum(hid * hid, axis=1, keepdims=True)
            mean = jnp.mean(hid, axis=1, keepdims=True)
            cen = hid - mean
            var = jnp.mean(cen * cen, axis=1, keepdims=True)
            att[at, :] = (cen / jnp.sqrt(var + 1e-6) * scale + shift).astype(bf16)
            return total

        total = lax.fori_loop(0, tok // step, body, jnp.zeros((step, 1), f32))
        sq_ref[r : r + 1, :] = jnp.broadcast_to(jnp.sum(total, axis=0, keepdims=True), (1, LANES))
        pred = lax.dot_general(
            fw_ref[...], att[r * tok : (r + 1) * tok, :], (((1,), (1,)), ((), ())), preferred_element_type=f32
        )
        cond = lax.axis_index("cfg") == 0
        pred_ref[r] = jnp.where(cond, guide_ref[r], 1.0 - guide_ref[r]) * pred


def finish(guidance, ra, rb, hidden_in, gate, mod, out_bias, final_weight, out_weight):
    shards, tok, _ = rb.shape
    width = out_weight.shape[0]
    c_out = final_weight.shape[0]
    n_pairs = width // LANES - shards
    vmem = pl.BlockSpec(memory_space=pltpu.VMEM)
    return pl.pallas_call(
        functools.partial(finish_kernel, n_pairs),
        in_specs=[pl.BlockSpec(memory_space=pltpu.SMEM)] + [vmem] * 7 + [pl.BlockSpec(memory_space=pl.ANY)],
        out_specs=[vmem, vmem],
        out_shape=[
            jax.ShapeDtypeStruct((2, c_out, tok), f32),
            jax.ShapeDtypeStruct((8, LANES), f32),
        ],
        scratch_shapes=[
            pltpu.VMEM((2 * tok, width), bf16),
            pltpu.VMEM((width, width), bf16),
            pltpu.VMEM((2 * tok, width), f32),
            pltpu.SemaphoreType.DMA((5,)),
        ],
        compiler_params=pltpu.CompilerParams(vmem_limit_bytes=40 * 1024 * 1024),
        cost_estimate=pl.CostEstimate(
            flops=4 * tok * width * (width + c_out), bytes_accessed=2 * width * width, transcendentals=0
        ),
        name="finish",
    )(guidance, ra, rb, hidden_in, gate, mod, out_bias, final_weight, out_weight)


def exchange(x, axis, size, combine):
    step = 1
    while step < size:
        x = combine(x, lax.ppermute(x, axis, [(i, i ^ step) for i in range(size)]))
        step *= 2
    return x


def local(
    latent, hidden_in, img_query, img_key, img_value, txt_key, txt_value, text_len, head_slot,
    out_weight, out_bias, attn_gate, final_mod, final_weight, final_bias, timesteps, guidance,
):
    shards = lax.axis_size("seq")
    position = lax.axis_index("seq")
    head_count = head_slot.shape[0]
    model_width = out_weight.shape[0]
    tok, txt = img_query.shape[2], txt_key.shape[2]
    image_rows = tok * shards
    per_shard = (head_count + shards - 1) // shards

    text = [x.transpose(0, 2, 1, 3) for x in (txt_key, txt_value)]
    streams = (img_query, img_key, img_value, *text)

    def swap(x):
        return lax.all_to_all(x, "seq", split_axis=0, concat_axis=0, tiled=True)

    in_c = swap(pack_single(*streams, shards))
    in_a = swap(pack_pairs(0, *streams, shards))
    out_c, top_c = attend(in_c, text_len, 2, tok, txt, True)
    second, out_c = lax.optimization_barrier((pack_pairs(1, *streams, shards), out_c))
    in_b = swap(second)
    out_a, top_a = attend(in_a, text_len, 0, tok, txt, False, out_c)
    back_a = swap(out_a)
    out_b, top_b = attend(in_b, text_len, 1, tok, txt, False)
    back_b = swap(out_b)

    pred, squares = finish(
        guidance, back_a, back_b, hidden_in, attn_gate, final_mod,
        out_bias[None], final_weight.T, out_weight,
    )
    velocity = pred + lax.ppermute(pred, "cfg", [(0, 1), (1, 0)]) + final_bias[None, :, None]
    step_size = (sigma_of(timesteps - 1) - sigma_of(timesteps))[:, None, None]
    latent_next = latent.transpose(0, 2, 1) + step_size * velocity
    velocity, latent_next = velocity.transpose(0, 2, 1), latent_next.transpose(0, 2, 1)

    lane = jnp.arange(LANES, dtype=jnp.int32)
    pair_top = jnp.maximum(top_a[0:2], top_b[0:2])
    single_top = jnp.maximum(top_c[0], top_c[1])
    single_head = 2 * shards + 2 * (position // 4) + position % 2
    table = jnp.full((LANES,), -jnp.inf, f32)
    table = jnp.where(lane == 2 * position, pair_top[0], table)
    table = jnp.where(lane == 2 * position + 1, pair_top[1], table)
    table = jnp.where((lane == single_head) & (single_head < head_count), single_top, table)
    table = exchange(table, "cfg", 2, jnp.maximum)
    table = exchange(table, "req", 4, jnp.maximum)

    small = jnp.where(lane == LANES - 2, squares[0], jnp.where(lane == LANES - 1, squares[1], table))

    def combine(a, b):
        return jnp.where(lane < LANES - 2, jnp.maximum(a, b), a + b)

    small = exchange(small, "seq", shards, combine)
    hidden_norms = jnp.sqrt(small[LANES - 2 :] / (image_rows * model_width))[None, :]

    own_slots = position * per_shard + jnp.arange(per_shard, dtype=jnp.int32)
    match = head_slot[None, :] == own_slots[:, None]
    best = jnp.max(jnp.where(match, small[None, :head_count], -jnp.inf), axis=1)
    max_logits = jnp.where(jnp.any(match, axis=1), best, 0.0)
    return (velocity, latent_next, hidden_norms, max_logits)


def solution(mesh):
    in_specs = (
        P("req", "seq", None),
        P("cfg", "req", "seq", None),
        P("cfg", "req", "seq", None),
        P("cfg", "req", "seq", None),
        P("cfg", "req", "seq", None),
        P("cfg", "req", "seq", None),
        P("cfg", "req", "seq", None),
        P("cfg", "req"),
        P(),
        P(),
        P(),
        P("cfg", "req", None),
        P("cfg", "req", None, None),
        P(),
        P(),
        P("req"),
        P("req"),
    )
    out_specs = (P("req", "seq", None), P("req", "seq", None), P("cfg", "req"), P("seq"))
    return jax.shard_map(local, mesh=mesh, in_specs=in_specs, out_specs=out_specs, check_vma=False)
```
